32 devices in a mesh: groups: 2 (over x), range: 16 (over z, y, core).
Axes of the slice: x: 2, y: 2, z: 4, core: 2. Of those that a mesh axis runs over, the one named last changes fastest.
Arguments:
- echoes: bfloat16 [4, 256, 16384], P('groups', 'range'), parts along dimension 0, may hold values from -6 to 6
- range_reference: float32 [2, 16384], replicated, may hold values from -6 to 6
- kernels: float32 [16, 8], replicated, may hold values from -2 to 2
- shifts: int32 [128, 256], P('range'), may hold values from 0 to 12
- phase_index: int32 [128, 256], P('range'), may hold values from 0 to 15
- centroid: int32 [128], P('range'), may hold values from 0 to 255
- azimuth_reference: float32 [2, 128, 256], P(None, 'range'), may hold values from -6 to 6
Outputs:
- focused_image: bfloat16 [4, 256, 16384], P('groups', None, 'range'), parts along dimension 0
The draws below stay inside these ranges and needn't reach their ends.
There are 2 independent parts, one for each index of `groups`. The reference program is written for one: setup_inputs(seed, part) draws one part's arguments, and reference() takes and returns one part's arrays. A program takes and returns all parts, laid end to end along the dimension named above; an argument that names none is the same for every part. Nothing has to cross between parts.
Inputs may be any that keep to these rules, and one draw needn't show every extreme that they name: `shifts`: whole range cells by which a block's energy at a Doppler bin has migrated. `phase_index`: row of kernels used by a block at a Doppler bin. `centroid`: doppler bins by which a block's azimuth reference is turned.
All inputs are finite; a program needn't handle non-finite values.
Results may differ from the reference program's by a relative error of at most 0.014.
Values may be sent and summed in bfloat16 or wider, within the bound.
No kernel may reach another device: no remote copies, remote signals or barrier semaphores. Data moves between devices by JAX's collectives and lax.ppermute only.
A program may use at most 128 MiB of HBM per device.

```python
import math
import jax
import jax.numpy as jnp
from jax import lax

NR = 16384
P_DEV = 16
NA = 256
R1 = 128
RB = 128
NBLK = 128
PHASES = 16
TAPS = 8
MAXSHIFT = 12
HALO = 16
N_RANGE = 16


def place_ends(values, own_key, smallest, high):
    longest = values.shape.index(max(values.shape))
    spots = []
    for shift in (0, 1):
        where = [jax.random.randint(jax.random.fold_in(own_key, axis), (), 0, length) for axis, length in enumerate(values.shape)]
        where[longest] = (where[longest] + shift) % values.shape[longest]
        spots.append(tuple(where))
    return values.at[spots[0]].set(smallest).at[spots[1]].set(high)


def block_scale(stream_key, extent, cuts, least, high):
    gain = 1.0
    for position, shards_of in cuts:
        steps = jax.random.uniform(jax.random.fold_in(jax.random.fold_in(stream_key, 6), position), (shards_of,), jnp.float32, least / len(cuts), high / len(cuts))
        gain = gain * jnp.repeat(jnp.exp(steps), extent[position] // shards_of).reshape((-1,) + (1,) * (len(extent) - 1 - position))
    return gain


def centred(rng, shape, scale, bound, shards=(), held_as=jnp.bfloat16):
    drawn = jax.random.normal(rng, shape, jnp.float32) * scale
    if len(shards) > 0:
        drawn = block_scale(rng, shape, shards, -0.22, 0.18) * drawn
    return jnp.clip(drawn, min=-bound, max=bound).astype(held_as)


def setup_inputs(seed: int = 0, part: int = 0) -> dict:
    seeds = jax.random.split(jax.random.key(seed), 8)
    own_keys = jax.random.split(jax.random.fold_in(seeds[7], part), 8)
    echoes = centred(own_keys[0], (2, NA, NR), 1.0, 6.0, ((1, 16),))
    range_reference = centred(seeds[1], (2, NR), 1.0, 6.0, (), jnp.float32)
    kernels = centred(seeds[2], (PHASES, TAPS), 0.35, 2.0, (), jnp.float32)
    shifts = place_ends(jax.random.randint(seeds[3], (NBLK, NA), 0, MAXSHIFT + 1), jax.random.fold_in(seeds[3], 1), 0, MAXSHIFT).astype(jnp.int32)
    phase_index = place_ends(jax.random.randint(seeds[4], (NBLK, NA), 0, PHASES), jax.random.fold_in(seeds[4], 1), 0, PHASES - 1).astype(jnp.int32)
    centroid = place_ends(jax.random.randint(seeds[5], (NBLK,), 0, NA), jax.random.fold_in(seeds[5], 1), 0, NA - 1).astype(jnp.int32)
    azimuth_reference = centred(seeds[6], (2, NBLK, NA), 1.0, 6.0, ((1, 16),), jnp.float32)
    return dict(echoes=echoes, range_reference=range_reference, kernels=kernels, shifts=shifts, phase_index=phase_index, centroid=centroid, azimuth_reference=azimuth_reference)


def transform_matrix(length, orient):
    number_line = jnp.arange(length, dtype=jnp.int32)
    angles = 2.0 * math.pi / length * (number_line[:, None] * number_line[None, :] % length).astype(jnp.float32)
    cosine = jnp.cos(angles)
    sine_part = orient * jnp.sin(angles)
    matrix = jnp.stack([jnp.stack([cosine, -sine_part], 1), jnp.stack([sine_part, cosine], 1)], 0)
    return matrix.astype(jnp.bfloat16)

def twiddle(first_len, second_len, orient, factor):
    first_axis = jnp.arange(first_len, dtype=jnp.int32)
    second_axis = jnp.arange(second_len, dtype=jnp.int32)
    whole = first_len * second_len
    angles = 2.0 * math.pi / whole * (first_axis[:, None] * second_axis[None, :] % whole).astype(jnp.float32)
    return (jnp.cos(angles) * factor, orient * jnp.sin(angles) * factor)

def complex_times(values, real_part, imag_part):
    return jnp.stack([values[0] * real_part - values[1] * imag_part, values[0] * imag_part + values[1] * real_part], 0)

def product_of(pattern, matrix, values):
    return jnp.einsum(pattern, matrix.astype(jnp.float32), values.astype(jnp.float32), precision=lax.Precision.HIGHEST)

def range_lines(pulse_lines, reference_slots, range_first, range_second):
    values = pulse_lines.reshape(2, -1, range_first, range_second)
    twist_real, twist_imag = twiddle(range_first, range_second, -1.0, 1.0 / math.sqrt(range_first))
    halfway = complex_times(product_of('oaib,ipbm->opam', transform_matrix(range_first, -1.0), values), twist_real, twist_imag).astype(jnp.bfloat16)
    spectrum = product_of('oaib,ipkb->opka', transform_matrix(range_second, -1.0), halfway) * (1.0 / math.sqrt(range_second))
    spectrum = complex_times(spectrum, reference_slots[0], reference_slots[1]).astype(jnp.bfloat16)
    back_real, back_imag = twiddle(range_first, range_second, 1.0, 1.0 / math.sqrt(range_second))
    halfway = complex_times(product_of('oaib,ipkb->opka', transform_matrix(range_second, 1.0), spectrum), back_real, back_imag).astype(jnp.bfloat16)
    result = product_of('oaib,ipbm->opam', transform_matrix(range_first, 1.0), halfway) * (1.0 / math.sqrt(range_first))
    return result.reshape(2, -1, range_first * range_second).astype(jnp.bfloat16)

def azimuth_forward(cell_block, azimuth_first, azimuth_second):
    values = cell_block.reshape(2, azimuth_first, azimuth_second, -1)
    twist_real, twist_imag = twiddle(azimuth_first, azimuth_second, -1.0, 1.0 / math.sqrt(azimuth_first))
    halfway = complex_times(product_of('oaib,ibmc->oamc', transform_matrix(azimuth_first, -1.0), values), twist_real[:, :, None], twist_imag[:, :, None]).astype(jnp.bfloat16)
    spectrum = product_of('oaib,ikbc->okac', transform_matrix(azimuth_second, -1.0), halfway) * (1.0 / math.sqrt(azimuth_second))
    return spectrum.astype(jnp.bfloat16)

def azimuth_inverse(spectrum, azimuth_first, azimuth_second):
    back_real, back_imag = twiddle(azimuth_first, azimuth_second, 1.0, 1.0 / math.sqrt(azimuth_second))
    halfway = complex_times(product_of('oaib,ikbc->okac', transform_matrix(azimuth_second, 1.0), spectrum), back_real[:, :, None], back_imag[:, :, None]).astype(jnp.bfloat16)
    result = product_of('oaib,ibmc->oamc', transform_matrix(azimuth_first, 1.0), halfway) * (1.0 / math.sqrt(azimuth_first))
    return result.reshape(2, azimuth_first * azimuth_second, -1).astype(jnp.bfloat16)

def reference(echoes, range_reference, kernels, shifts, phase_index, centroid, azimuth_reference):
    range_first = R1
    range_second = NR // R1
    azimuth_first = N_RANGE
    azimuth_second = P_DEV
    lead_taps = TAPS // 2 - 1
    reference_slots = range_reference.reshape(2, range_second, range_first).transpose(0, 2, 1)
    groups = echoes.reshape(2, azimuth_first, azimuth_second, NR).transpose(1, 0, 2, 3)
    compressed = lax.map(lambda pulse_lines: range_lines(pulse_lines, reference_slots, range_first, range_second), groups)
    compressed = compressed.transpose(1, 0, 2, 3).reshape(2, NA, NR)
    cell_blocks = compressed.reshape(2, NA, NBLK, RB).transpose(2, 0, 1, 3)
    spectra = lax.map(lambda cell_block: azimuth_forward(cell_block, azimuth_first, azimuth_second).reshape(2, NA, RB), cell_blocks)
    doppler = spectra.transpose(1, 2, 0, 3).reshape(2, NA, NR)
    padded = jnp.pad(doppler, ((0, 0), (0, 0), (HALO, HALO)))
    bin_of_slot = (jnp.arange(azimuth_first, dtype=jnp.int32)[:, None] + azimuth_first * jnp.arange(azimuth_second, dtype=jnp.int32)[None, :]).reshape(NA)
    cell_line = jnp.arange(RB, dtype=jnp.int32)

    def focus(block_index):
        window = lax.dynamic_slice_in_dim(padded, (block_index * RB).astype(jnp.int32), RB + 2 * HALO, 2)
        shift_rows = shifts[block_index][bin_of_slot]
        phase_rows = phase_index[block_index][bin_of_slot]
        weights = kernels[phase_rows]
        summed = jnp.zeros((2, NA, RB), jnp.float32)
        for tap_index in range(TAPS):
            where_from = (HALO - lead_taps + tap_index + cell_line[None, :] + shift_rows[:, None]).astype(jnp.int32)
            picked = jnp.take_along_axis(window, jnp.broadcast_to(where_from[None], (2, NA, RB)), axis=2)
            summed = summed + weights[:, tap_index][None, :, None] * picked.astype(jnp.float32)
        rolled = azimuth_reference[:, block_index][:, ((bin_of_slot - centroid[block_index]) % NA).astype(jnp.int32)]
        focused = complex_times(summed, rolled[0][:, None], rolled[1][:, None]).astype(jnp.bfloat16)
        return azimuth_inverse(focused.reshape(2, azimuth_first, azimuth_second, RB), azimuth_first, azimuth_second)
    images = lax.map(focus, jnp.arange(NBLK, dtype=jnp.int32))
    return images.transpose(1, 2, 0, 3).reshape(2, NA, NR)
```

```python
import functools
import math

import jax
import jax.numpy as jnp
import numpy as np
from jax import lax
from jax.experimental import pallas as pl
from jax.experimental.pallas import tpu as pltpu
from jax.sharding import PartitionSpec as P

R1 = 128
RB = 128
MAXSHIFT = 12
LANES = 128
SUB = 8
SLOT = 32
LEFT = 8
BF = jnp.bfloat16
F32 = jnp.float32


def rounded(values):
    return np.asarray(np.asarray(values, np.float32), BF).astype(np.float64)


def unit(rows, columns, length, orient):
    angles = 2.0 * math.pi / length * (np.outer(rows, columns) % length)
    return rounded(np.cos(angles)) + 1j * orient * rounded(np.sin(angles))


def turn(rows, columns, length, orient):
    angles = 2.0 * math.pi / length * (np.outer(rows, columns) % length)
    return np.exp(1j * orient * angles)


def real_form(matrix):
    return np.stack(
        [np.stack([matrix.real, -matrix.imag], 1), np.stack([matrix.imag, matrix.real], 1)], 0
    )


def as_bf(values):
    return np.asarray(np.asarray(values, np.float32), BF)


def planes(values):
    return np.asarray(np.stack([values.real, values.imag], 0), np.float32)


def dot(left, right):
    return jnp.dot(left, right, preferred_element_type=F32)


def dot_t(left, right):
    return lax.dot_general(left, right, (((1,), (1,)), ((), ())), preferred_element_type=F32)


def compress_kernel(
    dests, x_ref, e1_ref, t1_ref, w2_ref, r_ref, w3_ref, t3_ref, e4_ref, out_ref, s_in, s_out
):
    pulses = x_ref.shape[1]
    second = t1_ref.shape[2]
    first = R1
    blocks = first // dests
    scale = 1.0 / math.sqrt(first)
    for part in range(2):
        for n1 in range(first):
            s_in[part, pl.ds(n1 * pulses, pulses), :] = x_ref[
                part, :, n1 * second : (n1 + 1) * second
            ].astype(F32)

    def pair(group, carry):
        lines = []
        for k in range(2):
            p = group * 2 + k
            lines.append(
                jnp.concatenate(
                    [s_in[part, pl.ds(p, first, stride=pulses), :].astype(BF) for part in range(2)],
                    0,
                )
            )
        half = dot(e1_ref[...], jnp.concatenate(lines, 1))
        rows = []
        for k in range(2):
            re = half[:first, k * second : (k + 1) * second]
            im = half[first:, k * second : (k + 1) * second]
            tr, ti = t1_ref[0], t1_ref[1]
            rows.append(
                jnp.concatenate([(re * tr - im * ti).astype(BF), (re * ti + im * tr).astype(BF)], 1)
            )
        spec = dot(jnp.concatenate(rows, 0), w2_ref[...])
        rows = []
        for k in range(2):
            re = spec[k * first : (k + 1) * first, :second]
            im = spec[k * first : (k + 1) * first, second:]
            tr, ti = r_ref[0], r_ref[1]
            rows.append(
                jnp.concatenate([(re * tr - im * ti).astype(BF), (re * ti + im * tr).astype(BF)], 1)
            )
        back = dot(jnp.concatenate(rows, 0), w3_ref[...])
        lines = []
        for k in range(2):
            re = back[k * first : (k + 1) * first, :second]
            im = back[k * first : (k + 1) * first, second:]
            tr, ti = t3_ref[0], t3_ref[1]
            lines.append(
                jnp.concatenate([(re * tr - im * ti).astype(BF), (re * ti + im * tr).astype(BF)], 0)
            )
        done = dot(e4_ref[...], jnp.concatenate(lines, 1))
        for k in range(2):
            p = group * 2 + k
            s_out[pl.ds(pl.multiple_of(p * 2 * first, 2 * first), 2 * first), :] = (
                done[:, k * second : (k + 1) * second] * scale
            )
        return carry

    lax.fori_loop(0, pulses // 2, pair, 0)

    def tile(dest, part, block):
        row = (dest * 2 + part) * blocks + block
        return s_out[pl.ds(row, pulses, stride=2 * first), :]

    lane = lax.broadcasted_iota(jnp.int32, (SUB, LANES), 1)
    for dest in range(dests):
        for part in range(2):
            for block in range(blocks):
                row = (part * blocks + block) * pulses
                out_ref[dest, row : row + pulses, :] = tile(dest, part, block).astype(BF)
        halo = jnp.zeros((SUB, LANES), F32)
        for part in range(2):
            after = tile(dest + 1, part, 0) if dest + 1 < dests else None
            before = tile(dest - 1, part, blocks - 1) if dest > 0 else None
            for h in range(pulses // SUB):
                piece = jnp.zeros((SUB, LANES), F32)
                if after is not None:
                    piece = jnp.where(lane < 2 * SUB, after[h * SUB : (h + 1) * SUB], piece)
                if before is not None:
                    piece = jnp.where(lane >= LANES - 3, before[h * SUB : (h + 1) * SUB], piece)
                slot = part * (pulses // SUB) + h
                halo = halo + (pltpu.roll(piece, SLOT * slot, 1) if slot else piece)
        row = 2 * blocks * pulses
        out_ref[dest, row : row + SUB, :] = halo.astype(BF)


def params_kernel(ph_ref, k_ref, c_ref, a_ref, w_ref, ar_ref):
    blocks, bins = ph_ref.shape
    phases, taps = k_ref.shape
    phase = ph_ref[...]
    rows = [jnp.zeros((blocks, bins), F32) for _ in range(taps)]
    for q in range(phases):
        hit = phase == q
        for t in range(taps):
            rows[t] = jnp.where(hit, k_ref[q, t], rows[t])
    for t in range(taps):
        for h in range(bins // LANES):
            w_ref[t, h * blocks : (h + 1) * blocks, :] = rows[t][:, h * LANES : (h + 1) * LANES]
    for part in range(2):
        for b in range(blocks):
            line = pltpu.roll(a_ref[part, b : b + 1, :], c_ref[b], 1)
            for h in range(bins // LANES):
                ar_ref[part, h * blocks + b : h * blocks + b + 1, :] = line[
                    :, h * LANES : (h + 1) * LANES
                ]


def focus_kernel(y_ref, mf_ref, mi_ref, eye_ref, edge_ref, s_ref, w_ref, a_ref, out_ref, x_ref):
    sources = y_ref.shape[0]
    bins = out_ref.shape[1]
    cells = out_ref.shape[2]
    blocks = cells // RB
    pulses = bins // sources
    taps = w_ref.shape[0]
    halves = bins // LANES
    q_rows = halves * blocks
    stride = 2 * q_rows
    lead = taps // 2 - 1

    def put(jj, count, part, h, b, values):
        x_ref[pl.ds(jj * stride + part * q_rows + h * blocks + b, count, stride=stride), :] = values

    for first in range(0, blocks, 2):
        own = []
        for b in range(first, first + 2):
            own.append(
                jnp.concatenate(
                    [
                        y_ref[r, (o * blocks + b) * pulses : (o * blocks + b + 1) * pulses, :]
                        for r in range(sources)
                        for o in range(2)
                    ],
                    0,
                )
            )
        dop = dot(mf_ref[...], jnp.concatenate(own, 1)).astype(BF)
        turned = dot_t(eye_ref[...], dop)
        for k in range(2):
            b = first + k
            for part in range(2):
                for h in range(halves):
                    col = part * bins + h * LANES
                    here = turned[k * RB : (k + 1) * RB, col : col + LANES]
                    put(LEFT, RB, part, h, b, here)
                    if b > 0:
                        put(LEFT + RB, 2 * SUB, part, h, b - 1, here[: 2 * SUB])
                    if b + 1 < blocks:
                        put(0, LEFT, part, h, b + 1, here[RB - LEFT :])
    own = []
    for r in range(sources):
        held = y_ref[r, 2 * blocks * pulses : 2 * blocks * pulses + SUB, :].astype(F32)
        for o in range(2):
            for h in range(pulses // SUB):
                slot = o * (pulses // SUB) + h
                own.append(pltpu.roll(held, LANES - SLOT * slot, 1) if slot else held)
    dop = dot(mf_ref[...], jnp.concatenate(own, 0).astype(BF)).astype(BF)
    turned = dot_t(edge_ref[...], dop)
    for part in range(2):
        for h in range(halves):
            col = part * bins + h * LANES
            put(LEFT + RB, 2 * SUB, part, h, blocks - 1, turned[: 2 * SUB, col : col + LANES])
            put(0, LEFT, part, h, 0, turned[2 * SUB : 3 * SUB, col : col + LANES])

    for g in range(q_rows // SUB):
        shift = s_ref[g * SUB : (g + 1) * SUB, :]
        bits = [(shift & (1 << k)) != 0 for k in range(4)]
        weights = [w_ref[t, g * SUB : (g + 1) * SUB, :] for t in range(taps)]
        for part in range(2):
            base = part * q_rows + g * SUB
            seen = [{} for _ in range(5)]

            def moved(level, i):
                if i not in seen[level]:
                    if level == 0:
                        row = (i + LEFT - lead) * stride + base
                        seen[0][i] = x_ref[row : row + SUB, :]
                    else:
                        step = 1 << (level - 1)
                        seen[level][i] = jnp.where(
                            bits[level - 1], moved(level - 1, i + step), moved(level - 1, i)
                        )
                return seen[level][i]

            for j in range(RB):
                total = weights[0] * moved(4, j)
                for t in range(1, taps):
                    total = total + weights[t] * moved(4, j + t)
                x_ref[j * stride + base : j * stride + base + SUB, :] = total

    for first in range(0, blocks, 2):
        lines = []
        for b in range(first, first + 2):
            re_parts, im_parts = [], []
            for h in range(halves):
                q = h * blocks + b
                re = x_ref[pl.ds(q, RB, stride=stride), :]
                im = x_ref[pl.ds(q_rows + q, RB, stride=stride), :]
                ar = a_ref[0, q : q + 1, :]
                ai = a_ref[1, q : q + 1, :]
                re_parts.append((re * ar - im * ai).astype(BF))
                im_parts.append((re * ai + im * ar).astype(BF))
            lines.append(jnp.concatenate(re_parts + im_parts, 1))
        image = dot_t(mi_ref[...], jnp.concatenate(lines, 0)).astype(BF)
        for part in range(2):
            out_ref[part, :, first * RB : (first + 2) * RB] = image[part * bins : (part + 1) * bins]


def vmem(count):
    return [pl.BlockSpec(memory_space=pltpu.VMEM)] * count


def local(echoes, range_reference, kernels, shifts, phase_index, centroid, azimuth_reference):
    ranks = lax.axis_size("range")
    pulses, samples = echoes.shape[1:]
    first, second = R1, samples // R1
    cells = samples // ranks
    blocks = cells // RB
    bins = ranks * pulses
    taps = kernels.shape[1]
    halves = bins // LANES
    q_rows = halves * blocks
    assert second == RB and pulses == 2 * SUB and bins % LANES == 0 and blocks % 2 == 0

    n1, n2 = np.arange(first), np.arange(second)
    e1 = real_form(unit(n1, n1, first, -1.0)).reshape(2 * first, 2 * first)
    t1 = turn(n1, n2, samples, -1.0) / math.sqrt(first)
    w2 = real_form(unit(n2, n2, second, -1.0)).transpose(2, 3, 0, 1).reshape(2 * second, 2 * second)
    w3 = real_form(unit(n2, n2, second, 1.0)).transpose(2, 3, 0, 1).reshape(2 * second, 2 * second)
    t3 = turn(n1, n2, samples, 1.0) / math.sqrt(second)
    e4 = real_form(unit(n1, n1, first, 1.0)).reshape(2, ranks, blocks, 2 * first)
    e4 = e4.transpose(1, 0, 2, 3).reshape(2 * first, 2 * first)
    slots = range_reference.reshape(2, second, first).transpose(0, 2, 1) * (1.0 / math.sqrt(second))
    rows = 2 * blocks * pulses + SUB
    sent = pl.pallas_call(
        functools.partial(compress_kernel, ranks),
        out_shape=jax.ShapeDtypeStruct((ranks, rows, LANES), BF),
        in_specs=vmem(8),
        out_specs=pl.BlockSpec(memory_space=pltpu.VMEM),
        scratch_shapes=[
            pltpu.VMEM((2, first * pulses, second), F32),
            pltpu.VMEM((pulses * 2 * first, second), F32),
        ],
        compiler_params=pltpu.CompilerParams(vmem_limit_bytes=40 << 20),
        name="compress",
    )(echoes, as_bf(e1), planes(t1), as_bf(w2), slots, as_bf(w3), planes(t3), as_bf(e4))

    arrived = lax.all_to_all(sent, "range", 0, 0)

    weights, turned = pl.pallas_call(
        params_kernel,
        out_shape=(
            jax.ShapeDtypeStruct((taps, q_rows, LANES), F32),
            jax.ShapeDtypeStruct((2, q_rows, LANES), F32),
        ),
        in_specs=[
            pl.BlockSpec(memory_space=pltpu.VMEM),
            pl.BlockSpec(memory_space=pltpu.SMEM),
            pl.BlockSpec(memory_space=pltpu.SMEM),
            pl.BlockSpec(memory_space=pltpu.VMEM),
        ],
        out_specs=tuple(vmem(2)),
        name="params",
    )(phase_index, kernels, centroid, azimuth_reference)
    spots = shifts.reshape(blocks, halves, LANES).transpose(1, 0, 2).reshape(q_rows, LANES)

    f = np.arange(bins)
    k1, k2 = f % ranks, f // ranks
    r, p = np.arange(ranks), np.arange(pulses)
    ahead = (
        unit(k1, r, ranks, -1.0)[:, :, None]
        * (turn(k1, p, bins, -1.0) * unit(k2, p, pulses, -1.0))[:, None, :]
        / math.sqrt(bins)
    )
    ahead = real_form(ahead.reshape(bins, bins)).reshape(2 * bins, 2, ranks, pulses)
    ahead = ahead.transpose(0, 2, 1, 3).reshape(2 * bins, 2 * bins)
    behind = (
        unit(r, k1, ranks, 1.0)[:, None, :]
        * (turn(p, k1, bins, 1.0) * unit(p, k2, pulses, 1.0))[None, :, :]
        / math.sqrt(bins)
    )
    behind = real_form(behind.reshape(bins, bins)).reshape(2 * bins, 2 * bins)
    edge = np.zeros((SLOT, LANES))
    edge[: 2 * SUB, : 2 * SUB] = np.eye(2 * SUB)
    edge[2 * SUB : 3 * SUB, LANES - SUB :] = np.eye(SUB)
    span = LEFT + RB + 3 * SUB
    return pl.pallas_call(
        focus_kernel,
        out_shape=jax.ShapeDtypeStruct((2, bins, cells), BF),
        in_specs=vmem(8),
        out_specs=pl.BlockSpec(memory_space=pltpu.VMEM),
        scratch_shapes=[pltpu.VMEM((span * 2 * q_rows, LANES), F32)],
        compiler_params=pltpu.CompilerParams(vmem_limit_bytes=48 << 20),
        name="focus",
    )(
        arrived,
        as_bf(ahead),
        as_bf(behind),
        as_bf(np.eye(2 * RB)),
        as_bf(edge),
        spots,
        weights,
        turned,
    )


def solution(mesh):
    in_specs = (
        P("groups", "range", None),
        P(),
        P(),
        P("range", None),
        P("range", None),
        P("range"),
        P(None, "range", None),
    )
    out_specs = P("groups", None, "range")
    return jax.shard_map(local, mesh=mesh, in_specs=in_specs, out_specs=out_specs, check_vma=False)
```

```python
import functools
import math

import jax
import jax.numpy as jnp
import numpy as np
from jax import lax
from jax.experimental import pallas as pl
from jax.experimental.pallas import tpu as pltpu
from jax.sharding import PartitionSpec as P

R1 = 128
RB = 128
MAXSHIFT = 12
LANES = 128
SUB = 8
SLOT = 32
LEFT = 8
BF = jnp.bfloat16
F32 = jnp.float32
TAP = BF
AT_ONCE = 16


def rounded(values):
    return np.asarray(np.asarray(values, np.float32), BF).astype(np.float64)


def unit(rows, columns, length, orient):
    angles = 2.0 * math.pi / length * (np.outer(rows, columns) % length)
    return rounded(np.cos(angles)) + 1j * orient * rounded(np.sin(angles))


def turn(rows, columns, length, orient):
    angles = 2.0 * math.pi / length * (np.outer(rows, columns) % length)
    return np.exp(1j * orient * angles)


def real_form(matrix):
    return np.stack(
        [np.stack([matrix.real, -matrix.imag], 1), np.stack([matrix.imag, matrix.real], 1)], 0
    )


def as_bf(values):
    return np.asarray(np.asarray(values, np.float32), BF)


def planes(values):
    return np.asarray(np.stack([values.real, values.imag], 0), np.float32)


def dot(left, right):
    return jnp.dot(left, right, preferred_element_type=F32)


def dot_t(left, right):
    return lax.dot_general(left, right, (((1,), (1,)), ((), ())), preferred_element_type=F32)


def turned_by(values, table, axis):
    re, im = values
    tr, ti = table
    return jnp.concatenate([(re * tr - im * ti).astype(BF), (re * ti + im * tr).astype(BF)], axis)


def compress_kernel(
    dests, x_hbm, m_hbm, t_hbm, r_hbm, out_hbm, x_v, m_v, t_v, r_v, s_in, s_out, o_v, r_sq, in_sem, out_sem
):
    pulses = x_hbm.shape[1]
    samples = x_hbm.shape[2]
    first = R1
    second = samples // first
    blocks = first // dests
    scale = 1.0 / math.sqrt(first)
    gap_in = pulses + 1
    gap_out = 2 * first + 1
    parts = 2

    copies = [pltpu.make_async_copy(r_hbm, r_v, in_sem.at[0])]
    span = samples // parts
    for part in range(2):
        for k in range(parts):
            piece = pl.ds(k * span, span)
            copies.append(
                pltpu.make_async_copy(
                    x_hbm.at[part, :, piece], x_v.at[part, :, piece], in_sem.at[len(copies)]
                )
            )
    copies.append(pltpu.make_async_copy(m_hbm, m_v, in_sem.at[len(copies)]))
    copies.append(pltpu.make_async_copy(t_hbm, t_v, in_sem.at[len(copies)]))
    for copy in copies:
        copy.start()

    copies[0].wait()
    for k2 in range(second):
        r_sq[pl.ds(k2, 2, stride=second + 1), :] = r_v[:, k2 * first : (k2 + 1) * first]
    slots = []
    for part in range(2):
        row = part * (second + 1)
        slots.append(jnp.transpose(r_sq[row : row + second, :]) * (1.0 / math.sqrt(second)))
    for part in range(2):
        r_sq[part * first : (part + 1) * first, :] = slots[part]

    for part in range(2):
        for k in range(parts):
            copies[1 + part * parts + k].wait()
            for n1 in range(k * first // parts, (k + 1) * first // parts):
                row = (part * first + n1) * gap_in
                s_in[row : row + pulses, :] = x_v[part, :, n1 * second : (n1 + 1) * second].astype(
                    F32
                )
    copies[-2].wait()
    copies[-1].wait()

    for group in range(0, pulses, AT_ONCE):
        lines = []
        for p in range(group, group + AT_ONCE):
            lines.append(
                jnp.concatenate(
                    [
                        s_in[pl.ds(part * first * gap_in + p, first, stride=gap_in), :].astype(BF)
                        for part in range(2)
                    ],
                    0,
                )
            )
        half = dot(m_v[0], jnp.concatenate(lines, 1))
        table = (t_v[0], t_v[1])
        rows = []
        for k in range(AT_ONCE):
            cols = slice(k * second, (k + 1) * second)
            rows.append(turned_by((half[:first, cols], half[first:, cols]), table, 1))
        spec = dot(jnp.concatenate(rows, 0), m_v[1])
        table = (r_sq[:first, :], r_sq[first : 2 * first, :])
        rows = []
        for k in range(AT_ONCE):
            here = spec[k * first : (k + 1) * first]
            rows.append(turned_by((here[:, :second], here[:, second:]), table, 1))
        back = dot(jnp.concatenate(rows, 0), m_v[2])
        table = (t_v[2], t_v[3])
        lines = []
        for k in range(AT_ONCE):
            here = back[k * first : (k + 1) * first]
            lines.append(turned_by((here[:, :second], here[:, second:]), table, 0))
        done = dot(m_v[3], jnp.concatenate(lines, 1))
        for k in range(AT_ONCE):
            row = (group + k) * gap_out
            s_out[row : row + 2 * first, :] = done[:, k * second : (k + 1) * second] * scale

    def tile(dest, part, block):
        return s_out[pl.ds((dest * 2 + part) * blocks + block, pulses, stride=gap_out), :]

    lane = lax.broadcasted_iota(jnp.int32, (SUB, LANES), 1)
    sends = []
    for dest in range(dests):
        for part in range(2):
            for block in range(blocks):
                row = (part * blocks + block) * pulses
                o_v[dest, row : row + pulses, :] = tile(dest, part, block).astype(BF)
        halo = jnp.zeros((SUB, LANES), F32)
        for part in range(2):
            after = tile(dest + 1, part, 0) if dest + 1 < dests else None
            before = tile(dest - 1, part, blocks - 1) if dest > 0 else None
            for h in range(pulses // SUB):
                piece = jnp.zeros((SUB, LANES), F32)
                if after is not None:
                    piece = jnp.where(lane < 2 * SUB, after[h * SUB : (h + 1) * SUB], piece)
                if before is not None:
                    piece = jnp.where(lane >= LANES - 3, before[h * SUB : (h + 1) * SUB], piece)
                slot = part * (pulses // SUB) + h
                halo = halo + (pltpu.roll(piece, SLOT * slot, 1) if slot else piece)
        row = 2 * blocks * pulses
        o_v[dest, row : row + SUB, :] = halo.astype(BF)
        sends.append(pltpu.make_async_copy(o_v.at[dest], out_hbm.at[dest], out_sem.at[dest]))
        sends[-1].start()
    for send in sends:
        send.wait()


def focus_kernel(
    y_ref, mf_ref, mi_ref, eye_ref, edge_ref, s_ref, ph_ref, k_ref, c_ref, a_ref, out_ref, x_ref, ar_ref, d_ref
):
    sources = y_ref.shape[0]
    bins = out_ref.shape[1]
    cells = out_ref.shape[2]
    blocks = cells // RB
    pulses = bins // sources
    phases, taps = k_ref.shape
    halves = bins // LANES
    q_rows = halves * blocks
    stride = 2 * q_rows + 1
    lead = taps // 2 - 1

    for part in range(2):
        for b in range(blocks):
            line = pltpu.roll(a_ref[part, b : b + 1, :], c_ref[b], 1)
            for h in range(halves):
                q = h * blocks + b
                ar_ref[part, q : q + 1, :] = line[:, h * LANES : (h + 1) * LANES]

    def put(jj, count, part, h, b, values):
        x_ref[pl.ds(jj * stride + part * q_rows + h * blocks + b, count, stride=stride), :] = values

    own = []
    for b in range(blocks):
        own.append(
            jnp.concatenate(
                [
                    y_ref[r, (o * blocks + b) * pulses : (o * blocks + b + 1) * pulses, :]
                    for r in range(sources)
                    for o in range(2)
                ],
                0,
            )
        )
    side = []
    for r in range(sources):
        held = y_ref[r, 2 * blocks * pulses : 2 * blocks * pulses + SUB, :].astype(F32)
        for o in range(2):
            for h in range(pulses // SUB):
                slot = o * (pulses // SUB) + h
                side.append(pltpu.roll(held, LANES - SLOT * slot, 1) if slot else held)
    own.append(jnp.concatenate(side, 0).astype(BF))
    d_ref[...] = dot(mf_ref[...], jnp.concatenate(own, 1)).astype(BF)
    for first in range(0, blocks, 2):
        turned = dot_t(eye_ref[...], d_ref[:, first * RB : (first + 2) * RB])
        for k in range(2):
            b = first + k
            for part in range(2):
                for h in range(halves):
                    col = part * bins + h * LANES
                    here = turned[k * RB : (k + 1) * RB, col : col + LANES]
                    put(LEFT, RB, part, h, b, here)
                    if b > 0:
                        put(LEFT + RB, 2 * SUB, part, h, b - 1, here[: 2 * SUB])
                    if b + 1 < blocks:
                        put(0, LEFT, part, h, b + 1, here[RB - LEFT :])
    turned = dot_t(edge_ref[...], d_ref[:, cells:])
    for part in range(2):
        for h in range(halves):
            col = part * bins + h * LANES
            put(LEFT + RB, 2 * SUB, part, h, blocks - 1, turned[: 2 * SUB, col : col + LANES])
            put(0, LEFT, part, h, 0, turned[2 * SUB : 3 * SUB, col : col + LANES])

    high = SUB * (4 // jnp.dtype(TAP).itemsize)
    for g in range(q_rows // high):
        shift = s_ref[g * high : (g + 1) * high, :]
        phase = ph_ref[g * high : (g + 1) * high, :]
        weights = [jnp.zeros((high, LANES), F32) for _ in range(taps)]
        for q in range(phases):
            hit = phase == q
            for t in range(taps):
                weights[t] = jnp.where(hit, k_ref[q, t], weights[t])
        weights = [w.astype(TAP) for w in weights]
        if TAP == BF:
            shift = shift.astype(jnp.int16)
        bits = [(shift & (1 << k)) != 0 for k in range(4)]
        for part in range(2):
            base = part * q_rows + g * high
            seen = [{} for _ in range(5)]

            def moved(level, i):
                if i not in seen[level]:
                    if level == 0:
                        row = (i + LEFT - lead) * stride + base
                        seen[0][i] = x_ref[row : row + high, :].astype(TAP)
                    else:
                        step = 1 << (level - 1)
                        seen[level][i] = jnp.where(
                            bits[level - 1], moved(level - 1, i + step), moved(level - 1, i)
                        )
                return seen[level][i]

            for j in range(RB):
                total = weights[0] * moved(4, j)
                for t in range(1, taps):
                    total = total + weights[t] * moved(4, j + t)
                x_ref[j * stride + base : j * stride + base + high, :] = total.astype(F32)

    for first in range(0, blocks, 2):
        lines = []
        for b in range(first, first + 2):
            re_parts, im_parts = [], []
            for h in range(halves):
                q = h * blocks + b
                re = x_ref[pl.ds(q, RB, stride=stride), :]
                im = x_ref[pl.ds(q_rows + q, RB, stride=stride), :]
                ar = ar_ref[0, q : q + 1, :]
                ai = ar_ref[1, q : q + 1, :]
                re_parts.append((re * ar - im * ai).astype(BF))
                im_parts.append((re * ai + im * ar).astype(BF))
            lines.append(jnp.concatenate(re_parts + im_parts, 1))
        image = dot_t(mi_ref[...], jnp.concatenate(lines, 0)).astype(BF)
        for part in range(2):
            out_ref[part, :, first * RB : (first + 2) * RB] = image[part * bins : (part + 1) * bins]


def vmem(count):
    return [pl.BlockSpec(memory_space=pltpu.VMEM)] * count


def local(echoes, range_reference, kernels, shifts, phase_index, centroid, azimuth_reference):
    ranks = lax.axis_size("range")
    pulses, samples = echoes.shape[1:]
    first, second = R1, samples // R1
    cells = samples // ranks
    blocks = cells // RB
    bins = ranks * pulses
    taps = kernels.shape[1]
    halves = bins // LANES
    q_rows = halves * blocks
    assert second == RB and pulses == 2 * SUB and bins % LANES == 0 and blocks % 2 == 0

    n1, n2 = np.arange(first), np.arange(second)
    e1 = real_form(unit(n1, n1, first, -1.0)).reshape(2 * first, 2 * first)
    t1 = turn(n1, n2, samples, -1.0) / math.sqrt(first)
    w2 = real_form(unit(n2, n2, second, -1.0)).transpose(2, 3, 0, 1).reshape(2 * second, 2 * second)
    w3 = real_form(unit(n2, n2, second, 1.0)).transpose(2, 3, 0, 1).reshape(2 * second, 2 * second)
    t3 = turn(n1, n2, samples, 1.0) / math.sqrt(second)
    e4 = real_form(unit(n1, n1, first, 1.0)).reshape(2, ranks, blocks, 2 * first)
    e4 = e4.transpose(1, 0, 2, 3).reshape(2 * first, 2 * first)
    rows = 2 * blocks * pulses + SUB
    anywhere = pl.BlockSpec(memory_space=pl.ANY)
    sent = pl.pallas_call(
        functools.partial(compress_kernel, ranks),
        out_shape=jax.ShapeDtypeStruct((ranks, rows, LANES), BF),
        in_specs=[anywhere] * 4,
        out_specs=anywhere,
        scratch_shapes=[
            pltpu.VMEM((2, pulses, samples), BF),
            pltpu.VMEM((4, 2 * first, 2 * first), BF),
            pltpu.VMEM((4, first, second), F32),
            pltpu.VMEM((2, samples), F32),
            pltpu.VMEM((2 * first * (pulses + 1), second), F32),
            pltpu.VMEM((pulses * (2 * first + 1), second), F32),
            pltpu.VMEM((ranks, rows, LANES), BF),
            pltpu.VMEM((2 * first + SUB, second), F32),
            pltpu.SemaphoreType.DMA((8,)),
            pltpu.SemaphoreType.DMA((ranks,)),
        ],
        compiler_params=pltpu.CompilerParams(vmem_limit_bytes=60 << 20),
        name="compress",
    )(
        echoes,
        np.stack([as_bf(e1), as_bf(w2), as_bf(w3), as_bf(e4)]),
        np.concatenate([planes(t1), planes(t3)]),
        range_reference,
    )

    arrived = lax.all_to_all(sent, "range", 0, 0)

    def spread(table):
        return table.reshape(blocks, halves, LANES).transpose(1, 0, 2).reshape(q_rows, LANES)

    f = np.arange(bins)
    k1, k2 = f % ranks, f // ranks
    r, p = np.arange(ranks), np.arange(pulses)
    ahead = (
        unit(k1, r, ranks, -1.0)[:, :, None]
        * (turn(k1, p, bins, -1.0) * unit(k2, p, pulses, -1.0))[:, None, :]
        / math.sqrt(bins)
    )
    ahead = real_form(ahead.reshape(bins, bins)).reshape(2 * bins, 2, ranks, pulses)
    ahead = ahead.transpose(0, 2, 1, 3).reshape(2 * bins, 2 * bins)
    behind = (
        unit(r, k1, ranks, 1.0)[:, None, :]
        * (turn(p, k1, bins, 1.0) * unit(p, k2, pulses, 1.0))[None, :, :]
        / math.sqrt(bins)
    )
    behind = real_form(behind.reshape(bins, bins)).reshape(2 * bins, 2 * bins)
    edge = np.zeros((SLOT, LANES))
    edge[: 2 * SUB, : 2 * SUB] = np.eye(2 * SUB)
    edge[2 * SUB : 3 * SUB, LANES - SUB :] = np.eye(SUB)
    span = LEFT + RB + 3 * SUB
    return pl.pallas_call(
        focus_kernel,
        out_shape=jax.ShapeDtypeStruct((2, bins, cells), BF),
        in_specs=vmem(7)
        + [
            pl.BlockSpec(memory_space=pltpu.SMEM),
            pl.BlockSpec(memory_space=pltpu.SMEM),
            pl.BlockSpec(memory_space=pltpu.VMEM),
        ],
        out_specs=pl.BlockSpec(memory_space=pltpu.VMEM),
        scratch_shapes=[
            pltpu.VMEM((span * (2 * q_rows + 1), LANES), F32),
            pltpu.VMEM((2, q_rows, LANES), F32),
            pltpu.VMEM((2 * bins, cells + LANES), BF),
        ],
        compiler_params=pltpu.CompilerParams(vmem_limit_bytes=48 << 20),
        name="focus",
    )(
        arrived,
        as_bf(ahead),
        as_bf(behind),
        as_bf(np.eye(2 * RB)),
        as_bf(edge),
        spread(shifts),
        spread(phase_index),
        kernels,
        centroid,
        azimuth_reference,
    )


def solution(mesh):
    in_specs = (
        P("groups", "range", None),
        P(),
        P(),
        P("range", None),
        P("range", None),
        P("range"),
        P(None, "range", None),
    )
    out_specs = P("groups", None, "range")
    return jax.shard_map(local, mesh=mesh, in_specs=in_specs, out_specs=out_specs, check_vma=False)
```

```python
import functools
import math

import jax
import jax.numpy as jnp
import numpy as np
from jax import lax
from jax.experimental import pallas as pl
from jax.experimental.pallas import tpu as pltpu
from jax.sharding import PartitionSpec as P

R1 = 128
RB = 128
LANES = 128
SUB = 8
SLOT = 32
LEFT = 8
BF = jnp.bfloat16
F32 = jnp.float32
TAP = BF
AT_ONCE = 16


def rounded(values):
    return np.asarray(np.asarray(values, np.float32), BF).astype(np.float64)


def unit(rows, columns, length, orient):
    angles = 2.0 * math.pi / length * (np.outer(rows, columns) % length)
    return rounded(np.cos(angles)) + 1j * orient * rounded(np.sin(angles))


def turn(rows, columns, length, orient):
    angles = 2.0 * math.pi / length * (np.outer(rows, columns) % length)
    return np.exp(1j * orient * angles)


def real_form(matrix):
    return np.stack(
        [np.stack([matrix.real, -matrix.imag], 1), np.stack([matrix.imag, matrix.real], 1)], 0
    )


def as_bf(values):
    return np.asarray(np.asarray(values, np.float32), BF)


def planes(values):
    return np.asarray(np.stack([values.real, values.imag], 0), np.float32)


def dot(left, right):
    return jnp.dot(left, right, preferred_element_type=F32)


def dot_t(left, right):
    return lax.dot_general(left, right, (((1,), (1,)), ((), ())), preferred_element_type=F32)


def turned_by(values, table, axis):
    re, im = values
    tr, ti = table
    return jnp.concatenate([(re * tr - im * ti).astype(BF), (re * ti + im * tr).astype(BF)], axis)


def compress_kernel(dests, me_ref, x_hbm, m_hbm, t_hbm, r_hbm, *refs):
    outs = refs[:dests]
    x_v, m_v, t_v, r_v, s_in, s_out, o_v, r_sq, in_sem, out_sem = refs[dests:]
    me = me_ref[0]
    pulses = x_hbm.shape[1]
    samples = x_hbm.shape[2]
    first = R1
    second = samples // first
    blocks = first // dests
    scale = 1.0 / math.sqrt(first)
    gap_in = pulses + 1
    gap_out = 2 * first + 1
    parts = 2

    copies = [pltpu.make_async_copy(r_hbm, r_v, in_sem.at[0])]
    span = samples // parts
    for part in range(2):
        for k in range(parts):
            piece = pl.ds(k * span, span)
            copies.append(
                pltpu.make_async_copy(
                    x_hbm.at[part, :, piece], x_v.at[part, :, piece], in_sem.at[len(copies)]
                )
            )
    copies.append(pltpu.make_async_copy(m_hbm, m_v, in_sem.at[len(copies)]))
    copies.append(pltpu.make_async_copy(t_hbm, t_v, in_sem.at[len(copies)]))
    for copy in copies:
        copy.start()

    copies[0].wait()
    for k2 in range(second):
        r_sq[pl.ds(k2, 2, stride=second + 1), :] = r_v[:, k2 * first : (k2 + 1) * first]
    slots = []
    for part in range(2):
        row = part * (second + 1)
        slots.append(jnp.transpose(r_sq[row : row + second, :]) * (1.0 / math.sqrt(second)))
    for part in range(2):
        r_sq[part * first : (part + 1) * first, :] = slots[part]

    for part in range(2):
        for k in range(parts):
            copies[1 + part * parts + k].wait()
            for n1 in range(k * first // parts, (k + 1) * first // parts):
                row = (part * first + n1) * gap_in
                s_in[row : row + pulses, :] = x_v[part, :, n1 * second : (n1 + 1) * second].astype(
                    F32
                )
    copies[-2].wait()
    copies[-1].wait()

    for group in range(0, pulses, AT_ONCE):
        lines = []
        for p in range(group, group + AT_ONCE):
            lines.append(
                jnp.concatenate(
                    [
                        s_in[pl.ds(part * first * gap_in + p, first, stride=gap_in), :].astype(BF)
                        for part in range(2)
                    ],
                    0,
                )
            )
        half = dot(m_v[0], jnp.concatenate(lines, 1))
        table = (t_v[0], t_v[1])
        rows = []
        for k in range(AT_ONCE):
            cols = slice(k * second, (k + 1) * second)
            rows.append(turned_by((half[:first, cols], half[first:, cols]), table, 1))
        spec = dot(jnp.concatenate(rows, 0), m_v[1])
        table = (r_sq[:first, :], r_sq[first : 2 * first, :])
        rows = []
        for k in range(AT_ONCE):
            here = spec[k * first : (k + 1) * first]
            rows.append(turned_by((here[:, :second], here[:, second:]), table, 1))
        back = dot(jnp.concatenate(rows, 0), m_v[2])
        table = (t_v[2], t_v[3])
        lines = []
        for k in range(AT_ONCE):
            here = back[k * first : (k + 1) * first]
            lines.append(turned_by((here[:, :second], here[:, second:]), table, 0))
        done = dot(m_v[3], jnp.concatenate(lines, 1))
        for k in range(AT_ONCE):
            row = (group + k) * gap_out
            s_out[row : row + 2 * first, :] = done[:, k * second : (k + 1) * second] * scale

    def tile(dest, part, block):
        return s_out[pl.ds((dest * 2 + part) * blocks + block, pulses, stride=gap_out), :]

    lane = lax.broadcasted_iota(jnp.int32, (SUB, LANES), 1)
    sends = []
    for k in reversed(range(dests)):
        dest = me ^ k
        for part in range(2):
            for block in range(blocks):
                row = (part * blocks + block) * pulses
                o_v[k, row : row + pulses, :] = tile(dest, part, block).astype(BF)
        halo = jnp.zeros((SUB, LANES), F32)
        take = (lane < 2 * SUB) & (dest + 1 < dests)
        give = (lane >= LANES - 3) & (dest > 0)
        for part in range(2):
            after = tile(jnp.minimum(dest + 1, dests - 1), part, 0)
            before = tile(jnp.maximum(dest - 1, 0), part, blocks - 1)
            for h in range(pulses // SUB):
                rows = slice(h * SUB, (h + 1) * SUB)
                piece = jnp.where(take, after[rows], jnp.where(give, before[rows], 0.0))
                slot = part * (pulses // SUB) + h
                halo = halo + (pltpu.roll(piece, SLOT * slot, 1) if slot else piece)
        row = 2 * blocks * pulses
        o_v[k, row : row + SUB, :] = halo.astype(BF)
        sends.append(pltpu.make_async_copy(o_v.at[k], outs[k], out_sem.at[k]))
        sends[-1].start()
    for send in sends:
        send.wait()


def focus_kernel(sources, *refs):
    y_refs = refs[:sources]
    mf_ref, mi_ref, eye_ref, edge_ref, s_ref, ph_ref, k_ref, c_ref, a_ref = refs[sources:-4]
    out_ref, x_ref, ar_ref, d_ref = refs[-4:]
    bins = out_ref.shape[1]
    cells = out_ref.shape[2]
    blocks = cells // RB
    pulses = bins // sources
    phases, taps = k_ref.shape
    halves = bins // LANES
    q_rows = halves * blocks
    stride = 2 * q_rows + 1
    lead = taps // 2 - 1

    for part in range(2):
        for b in range(blocks):
            line = pltpu.roll(a_ref[part, b : b + 1, :], c_ref[b], 1)
            for h in range(halves):
                q = h * blocks + b
                ar_ref[part, q : q + 1, :] = line[:, h * LANES : (h + 1) * LANES]

    def put(jj, count, part, h, b, values):
        x_ref[pl.ds(jj * stride + part * q_rows + h * blocks + b, count, stride=stride), :] = values

    own = []
    for b in range(blocks):
        own.append(
            jnp.concatenate(
                [
                    y_refs[r][(o * blocks + b) * pulses : (o * blocks + b + 1) * pulses, :]
                    for r in range(sources)
                    for o in range(2)
                ],
                0,
            )
        )
    side = []
    for r in range(sources):
        held = y_refs[r][2 * blocks * pulses : 2 * blocks * pulses + SUB, :].astype(F32)
        for o in range(2):
            for h in range(pulses // SUB):
                slot = o * (pulses // SUB) + h
                side.append(pltpu.roll(held, LANES - SLOT * slot, 1) if slot else held)
    own.append(jnp.concatenate(side, 0).astype(BF))
    d_ref[...] = dot(mf_ref[...], jnp.concatenate(own, 1)).astype(BF)
    for first in range(0, blocks, 2):
        turned = dot_t(eye_ref[...], d_ref[:, first * RB : (first + 2) * RB])
        for k in range(2):
            b = first + k
            for part in range(2):
                for h in range(halves):
                    col = part * bins + h * LANES
                    here = turned[k * RB : (k + 1) * RB, col : col + LANES]
                    put(LEFT, RB, part, h, b, here)
                    if b > 0:
                        put(LEFT + RB, 2 * SUB, part, h, b - 1, here[: 2 * SUB])
                    if b + 1 < blocks:
                        put(0, LEFT, part, h, b + 1, here[RB - LEFT :])
    turned = dot_t(edge_ref[...], d_ref[:, cells:])
    for part in range(2):
        for h in range(halves):
            col = part * bins + h * LANES
            put(LEFT + RB, 2 * SUB, part, h, blocks - 1, turned[: 2 * SUB, col : col + LANES])
            put(0, LEFT, part, h, 0, turned[2 * SUB : 3 * SUB, col : col + LANES])

    high = SUB * (4 // jnp.dtype(TAP).itemsize)
    for g in range(q_rows // high):
        shift = s_ref[g * high : (g + 1) * high, :]
        phase = ph_ref[g * high : (g + 1) * high, :]
        weights = [jnp.zeros((high, LANES), F32) for _ in range(taps)]
        for q in range(phases):
            hit = phase == q
            for t in range(taps):
                weights[t] = jnp.where(hit, k_ref[q, t], weights[t])
        weights = [w.astype(TAP) for w in weights]
        if TAP == BF:
            shift = shift.astype(jnp.int16)
        bits = [(shift & (1 << k)) != 0 for k in range(4)]
        for part in range(2):
            base = part * q_rows + g * high
            seen = [{} for _ in range(5)]

            def moved(level, i):
                if i not in seen[level]:
                    if level == 0:
                        row = (i + LEFT - lead) * stride + base
                        seen[0][i] = x_ref[row : row + high, :].astype(TAP)
                    else:
                        step = 1 << (level - 1)
                        seen[level][i] = jnp.where(
                            bits[level - 1], moved(level - 1, i + step), moved(level - 1, i)
                        )
                return seen[level][i]

            for j in range(RB):
                total = weights[0] * moved(4, j)
                for t in range(1, taps):
                    total = total + weights[t] * moved(4, j + t)
                x_ref[j * stride + base : j * stride + base + high, :] = total.astype(F32)

    for first in range(0, blocks, 2):
        lines = []
        for b in range(first, first + 2):
            re_parts, im_parts = [], []
            for h in range(halves):
                q = h * blocks + b
                re = x_ref[pl.ds(q, RB, stride=stride), :]
                im = x_ref[pl.ds(q_rows + q, RB, stride=stride), :]
                ar = ar_ref[0, q : q + 1, :]
                ai = ar_ref[1, q : q + 1, :]
                re_parts.append((re * ar - im * ai).astype(BF))
                im_parts.append((re * ai + im * ar).astype(BF))
            lines.append(jnp.concatenate(re_parts + im_parts, 1))
        image = dot_t(mi_ref[...], jnp.concatenate(lines, 0)).astype(BF)
        for part in range(2):
            out_ref[part, :, first * RB : (first + 2) * RB] = image[part * bins : (part + 1) * bins]


def order_of(ranks):
    far = [k for k in range(ranks) if k >= ranks // 2]
    near = [k for k in reversed(range(ranks)) if 0 < k < ranks // 2]
    order = []
    while far or near:
        order += far[:2] + near[:1]
        far, near = far[2:], near[1:]
    return order


def vmem(count):
    return [pl.BlockSpec(memory_space=pltpu.VMEM)] * count


def local(echoes, range_reference, kernels, shifts, phase_index, centroid, azimuth_reference):
    ranks = lax.axis_size("range")
    pulses, samples = echoes.shape[1:]
    first, second = R1, samples // R1
    cells = samples // ranks
    blocks = cells // RB
    bins = ranks * pulses
    halves = bins // LANES
    q_rows = halves * blocks
    assert second == RB and pulses == 2 * SUB and bins % LANES == 0 and blocks % 2 == 0

    n1, n2 = np.arange(first), np.arange(second)
    e1 = real_form(unit(n1, n1, first, -1.0)).reshape(2 * first, 2 * first)
    t1 = turn(n1, n2, samples, -1.0) / math.sqrt(first)
    w2 = real_form(unit(n2, n2, second, -1.0)).transpose(2, 3, 0, 1).reshape(2 * second, 2 * second)
    w3 = real_form(unit(n2, n2, second, 1.0)).transpose(2, 3, 0, 1).reshape(2 * second, 2 * second)
    t3 = turn(n1, n2, samples, 1.0) / math.sqrt(second)
    e4 = real_form(unit(n1, n1, first, 1.0)).reshape(2, ranks, blocks, 2 * first)
    e4 = e4.transpose(1, 0, 2, 3).reshape(2 * first, 2 * first)
    rows = 2 * blocks * pulses + SUB
    anywhere = pl.BlockSpec(memory_space=pl.ANY)
    sent = pl.pallas_call(
        functools.partial(compress_kernel, ranks),
        out_shape=[jax.ShapeDtypeStruct((rows, LANES), BF)] * ranks,
        in_specs=[pl.BlockSpec(memory_space=pltpu.SMEM)] + [anywhere] * 4,
        out_specs=[anywhere] * ranks,
        scratch_shapes=[
            pltpu.VMEM((2, pulses, samples), BF),
            pltpu.VMEM((4, 2 * first, 2 * first), BF),
            pltpu.VMEM((4, first, second), F32),
            pltpu.VMEM((2, samples), F32),
            pltpu.VMEM((2 * first * (pulses + 1), second), F32),
            pltpu.VMEM((pulses * (2 * first + 1), second), F32),
            pltpu.VMEM((ranks, rows, LANES), BF),
            pltpu.VMEM((2 * first + SUB, second), F32),
            pltpu.SemaphoreType.DMA((8,)),
            pltpu.SemaphoreType.DMA((ranks,)),
        ],
        compiler_params=pltpu.CompilerParams(vmem_limit_bytes=60 << 20),
        name="compress",
    )(
        lax.axis_index("range").astype(jnp.int32).reshape(1),
        echoes,
        np.stack([as_bf(e1), as_bf(w2), as_bf(w3), as_bf(e4)]),
        np.concatenate([planes(t1), planes(t3)]),
        range_reference,
    )

    arrived = [sent[0]] * ranks
    for k in order_of(ranks):
        arrived[k] = lax.ppermute(sent[k], "range", [(i, i ^ k) for i in range(ranks)])

    def spread(table):
        return table.reshape(blocks, halves, LANES).transpose(1, 0, 2).reshape(q_rows, LANES)

    f = np.arange(bins)
    k1, k2 = f % ranks, f // ranks
    r, p = np.arange(ranks), np.arange(pulses)
    ahead = (
        unit(k1, r, ranks, -1.0)[:, :, None]
        * (turn(k1, p, bins, -1.0) * unit(k2, p, pulses, -1.0))[:, None, :]
        / math.sqrt(bins)
    )
    ahead = real_form(ahead.reshape(bins, bins)).reshape(2 * bins, 2, ranks, pulses)
    ahead = ahead.transpose(0, 2, 1, 3).reshape(2 * bins, 2 * bins)
    behind = (
        unit(r, k1, ranks, 1.0)[:, None, :]
        * (turn(p, k1, bins, 1.0) * unit(p, k2, pulses, 1.0))[None, :, :]
        / math.sqrt(bins)
    )
    behind = real_form(behind.reshape(bins, bins)).reshape(2 * bins, 2 * bins)
    column = jnp.arange(2 * bins, dtype=jnp.int32)
    wanted = column ^ (lax.axis_index("range").astype(jnp.int32) * (2 * pulses))
    choose = (column[:, None] == wanted[None, :]).astype(BF)
    ahead = jnp.dot(as_bf(ahead), choose, preferred_element_type=F32).astype(BF)
    edge = np.zeros((SLOT, LANES))
    edge[: 2 * SUB, : 2 * SUB] = np.eye(2 * SUB)
    edge[2 * SUB : 3 * SUB, LANES - SUB :] = np.eye(SUB)
    span = LEFT + RB + 3 * SUB
    return pl.pallas_call(
        functools.partial(focus_kernel, ranks),
        out_shape=jax.ShapeDtypeStruct((2, bins, cells), BF),
        in_specs=vmem(6 + ranks)
        + [
            pl.BlockSpec(memory_space=pltpu.SMEM),
            pl.BlockSpec(memory_space=pltpu.SMEM),
            pl.BlockSpec(memory_space=pltpu.VMEM),
        ],
        out_specs=pl.BlockSpec(memory_space=pltpu.VMEM),
        scratch_shapes=[
            pltpu.VMEM((span * (2 * q_rows + 1), LANES), F32),
            pltpu.VMEM((2, q_rows, LANES), F32),
            pltpu.VMEM((2 * bins, cells + LANES), BF),
        ],
        compiler_params=pltpu.CompilerParams(vmem_limit_bytes=48 << 20),
        name="focus",
    )(
        *arrived,
        ahead,
        as_bf(behind),
        as_bf(np.eye(2 * RB)),
        as_bf(edge),
        spread(shifts),
        spread(phase_index),
        kernels,
        lax.rem(centroid, jnp.int32(bins)),
        azimuth_reference,
    )


def solution(mesh):
    in_specs = (
        P("groups", "range", None),
        P(),
        P(),
        P("range", None),
        P("range", None),
        P("range"),
        P(None, "range", None),
    )
    out_specs = P("groups", None, "range")

    return jax.shard_map(local, mesh=mesh, in_specs=in_specs, out_specs=out_specs, check_vma=False)
```

```python
import functools
import math

import jax
import jax.numpy as jnp
import numpy as np
from jax import lax
from jax.experimental import pallas as pl
from jax.experimental.pallas import tpu as pltpu
from jax.sharding import PartitionSpec as P

R1 = 128
RB = 128
LANES = 128
SUB = 8
SLOT = 32
LEFT = 8
BF = jnp.bfloat16
F32 = jnp.float32
CHUNK = 4
AT_ONCE = 16


def rounded(values):
    return np.asarray(np.asarray(values, np.float32), BF).astype(np.float64)


def unit(rows, columns, length, orient):
    angles = 2.0 * math.pi / length * (np.outer(rows, columns) % length)
    return rounded(np.cos(angles)) + 1j * orient * rounded(np.sin(angles))


def turn(rows, columns, length, orient):
    angles = 2.0 * math.pi / length * (np.outer(rows, columns) % length)
    return np.exp(1j * orient * angles)


def real_form(matrix):
    return np.stack(
        [np.stack([matrix.real, -matrix.imag], 1), np.stack([matrix.imag, matrix.real], 1)], 0
    )


def as_bf(values):
    return np.asarray(np.asarray(values, np.float32), BF)


def planes(values):
    return np.asarray(np.stack([values.real, values.imag], 0), np.float32)


def dot(left, right):
    return jnp.dot(left, right, preferred_element_type=F32)


def dot_t(left, right):
    return lax.dot_general(left, right, (((1,), (1,)), ((), ())), preferred_element_type=F32)


def turned_by(values, table, axis):
    re, im = values
    tr, ti = table
    return jnp.concatenate([(re * tr - im * ti).astype(BF), (re * ti + im * tr).astype(BF)], axis)


def compress_kernel(dests, me_ref, x_hbm, m_hbm, t_hbm, r_hbm, *refs):
    outs = refs[:dests]
    x_v, m_v, t_v, r_v, s_in, s_out, r_sq, in_sem = refs[dests:]
    me = me_ref[0]
    pulses = x_hbm.shape[1]
    samples = x_hbm.shape[2]
    first = R1
    second = samples // first
    blocks = first // dests
    scale = 1.0 / math.sqrt(first)
    gap_in = pulses + 1
    gap_out = 2 * first + 1
    parts = 2

    copies = [pltpu.make_async_copy(r_hbm, r_v, in_sem.at[0])]
    span = samples // parts
    for part in range(2):
        for k in range(parts):
            piece = pl.ds(k * span, span)
            copies.append(
                pltpu.make_async_copy(
                    x_hbm.at[part, :, piece], x_v.at[part, :, piece], in_sem.at[len(copies)]
                )
            )
    copies.append(pltpu.make_async_copy(m_hbm, m_v, in_sem.at[len(copies)]))
    copies.append(pltpu.make_async_copy(t_hbm, t_v, in_sem.at[len(copies)]))
    for copy in copies:
        copy.start()

    copies[0].wait()
    for k2 in range(second):
        r_sq[pl.ds(k2, 2, stride=second + 1), :] = r_v[:, k2 * first : (k2 + 1) * first]
    slots = []
    for part in range(2):
        row = part * (second + 1)
        slots.append(jnp.transpose(r_sq[row : row + second, :]) * (1.0 / math.sqrt(second)))
    for part in range(2):
        r_sq[part * first : (part + 1) * first, :] = slots[part]

    for part in range(2):
        for k in range(parts):
            copies[1 + part * parts + k].wait()
            for n1 in range(k * first // parts, (k + 1) * first // parts):
                row = (part * first + n1) * gap_in
                s_in[row : row + pulses, :] = x_v[part, :, n1 * second : (n1 + 1) * second].astype(
                    F32
                )
    copies[-2].wait()
    copies[-1].wait()

    for group in range(0, pulses, AT_ONCE):
        lines = []
        for p in range(group, group + AT_ONCE):
            lines.append(
                jnp.concatenate(
                    [
                        s_in[pl.ds(part * first * gap_in + p, first, stride=gap_in), :].astype(BF)
                        for part in range(2)
                    ],
                    0,
                )
            )
        half = dot(m_v[0], jnp.concatenate(lines, 1))
        table = (t_v[0], t_v[1])
        rows = []
        for k in range(AT_ONCE):
            cols = slice(k * second, (k + 1) * second)
            rows.append(turned_by((half[:first, cols], half[first:, cols]), table, 1))
        spec = dot(jnp.concatenate(rows, 0), m_v[1])
        table = (r_sq[:first, :], r_sq[first : 2 * first, :])
        rows = []
        for k in range(AT_ONCE):
            here = spec[k * first : (k + 1) * first]
            rows.append(turned_by((here[:, :second], here[:, second:]), table, 1))
        back = dot(jnp.concatenate(rows, 0), m_v[2])
        table = (t_v[2], t_v[3])
        lines = []
        for k in range(AT_ONCE):
            here = back[k * first : (k + 1) * first]
            lines.append(turned_by((here[:, :second], here[:, second:]), table, 0))
        done = dot(m_v[3], jnp.concatenate(lines, 1))
        for k in range(AT_ONCE):
            row = (group + k) * gap_out
            s_out[row : row + 2 * first, :] = done[:, k * second : (k + 1) * second] * scale

    def tile(dest, part, block):
        return s_out[pl.ds((dest * 2 + part) * blocks + block, pulses, stride=gap_out), :]

    lane = lax.broadcasted_iota(jnp.int32, (SUB, LANES), 1)
    for k in reversed(range(dests)):
        dest = me ^ k
        for part in range(2):
            for block in range(blocks):
                row = (part * blocks + block) * pulses
                outs[k][row : row + pulses, :] = tile(dest, part, block).astype(BF)
        halo = jnp.zeros((SUB, LANES), F32)
        take = (lane < 2 * SUB) & (dest + 1 < dests)
        give = (lane >= LANES - 3) & (dest > 0)
        for part in range(2):
            after = tile(jnp.minimum(dest + 1, dests - 1), part, 0)
            before = tile(jnp.maximum(dest - 1, 0), part, blocks - 1)
            for h in range(pulses // SUB):
                rows = slice(h * SUB, (h + 1) * SUB)
                piece = jnp.where(take, after[rows], jnp.where(give, before[rows], 0.0))
                slot = part * (pulses // SUB) + h
                halo = halo + (pltpu.roll(piece, SLOT * slot, 1) if slot else piece)
        row = 2 * blocks * pulses
        outs[k][row : row + SUB, :] = halo.astype(BF)


def params_kernel(ph_ref, k_ref, c_ref, a_ref, w_ref, t_ref):
    phases, taps = k_ref.shape
    blocks = a_ref.shape[1]
    phase = ph_ref[...]
    weights = [jnp.zeros(phase.shape, F32) for _ in range(taps)]
    for q in range(phases):
        hit = phase == q
        for t in range(taps):
            weights[t] = jnp.where(hit, k_ref[q, t], weights[t])
    for t in range(taps):
        w_ref[t] = weights[t]
    for part in range(2):
        for b in range(blocks):
            line = pltpu.roll(a_ref[part, b : b + 1, :], c_ref[b], 1)
            for h in range(phase.shape[0] // blocks):
                q = h * blocks + b
                t_ref[part, q : q + 1, :] = line[:, h * LANES : (h + 1) * LANES]


def focus_kernel(sources, *refs):
    y_refs = refs[:sources]
    mf_ref, mi_ref, edge_ref, s_ref, w_ref, a_ref = refs[sources : sources + 6]
    out_hbm, x_ref, d_ref, o_v, out_sem = refs[sources + 6 :]
    bins = out_hbm.shape[1]
    cells = out_hbm.shape[2]
    blocks = cells // RB
    pulses = bins // sources
    taps = w_ref.shape[0]
    halves = bins // LANES
    q_rows = halves * blocks
    stride = 2 * q_rows + 1
    lead = taps // 2 - 1

    def put(jj, count, part, h, b, values):
        x_ref[pl.ds(jj * stride + part * q_rows + h * blocks + b, count, stride=stride), :] = values

    own = []
    for b in range(blocks):
        own.append(
            jnp.concatenate(
                [
                    y[(o * blocks + b) * pulses : (o * blocks + b + 1) * pulses, :]
                    for y in y_refs
                    for o in range(2)
                ],
                0,
            )
        )
    side = []
    for y in y_refs:
        held = y[2 * blocks * pulses : 2 * blocks * pulses + SUB, :].astype(F32)
        for o in range(2):
            for h in range(pulses // SUB):
                slot = o * (pulses // SUB) + h
                side.append(pltpu.roll(held, LANES - SLOT * slot, 1) if slot else held)
    own.append(jnp.concatenate(side, 0).astype(BF))
    d_ref[...] = dot(mf_ref[...], jnp.concatenate(own, 1)).astype(BF)
    for b in range(blocks):
        for part in range(2):
            for h in range(halves):
                row = part * bins + h * LANES
                here = jnp.transpose(d_ref[row : row + LANES, b * RB : (b + 1) * RB]).astype(F32)
                put(LEFT, RB, part, h, b, here)
                if b > 0:
                    put(LEFT + RB, 2 * SUB, part, h, b - 1, here[: 2 * SUB])
                if b + 1 < blocks:
                    put(0, LEFT, part, h, b + 1, here[RB - LEFT :])
    turned = dot_t(edge_ref[...], d_ref[:, cells:])
    for part in range(2):
        for h in range(halves):
            col = part * bins + h * LANES
            put(LEFT + RB, 2 * SUB, part, h, blocks - 1, turned[: 2 * SUB, col : col + LANES])
            put(0, LEFT, part, h, 0, turned[2 * SUB : 3 * SUB, col : col + LANES])

    high = 2 * SUB
    for g in range(q_rows // high):
        shift = s_ref[g * high : (g + 1) * high, :].astype(jnp.int16)
        weights = [w_ref[t, g * high : (g + 1) * high, :].astype(BF) for t in range(taps)]
        ar, ai = [a_ref[part, g * high : (g + 1) * high, :].astype(BF) for part in range(2)]
        bits = [(shift & (1 << k)) != 0 for k in range(4)]
        seen = [[{} for _ in range(5)] for _ in range(2)]

        def moved(part, level, i):
            here = seen[part][level]
            if i not in here:
                if level == 0:
                    row = (i + LEFT - lead) * stride + part * q_rows + g * high
                    here[i] = x_ref[row : row + high, :].astype(BF)
                else:
                    step = 1 << (level - 1)
                    here[i] = jnp.where(
                        bits[level - 1], moved(part, level - 1, i + step), moved(part, level - 1, i)
                    )
            return here[i]

        for first in range(0, RB, CHUNK):
            sums = []
            for part in range(2):
                for j in range(first, first + CHUNK):
                    total = weights[0] * moved(part, 4, j)
                    for t in range(1, taps):
                        total = total + weights[t] * moved(part, 4, j + t)
                    sums.append(total)
            for k in range(CHUNK):
                re, im = sums[k], sums[CHUNK + k]
                row = (first + k) * stride + g * high
                x_ref[row : row + high, :] = (re * ar - im * ai).astype(F32)
                row += q_rows
                x_ref[row : row + high, :] = (re * ai + im * ar).astype(F32)

    sends = []
    for first in range(0, blocks, 2):
        lines = []
        for b in range(first, first + 2):
            lines.append(
                jnp.concatenate(
                    [
                        x_ref[pl.ds(part * q_rows + h * blocks + b, RB, stride=stride), :].astype(BF)
                        for part in range(2)
                        for h in range(halves)
                    ],
                    1,
                )
            )
        image = dot_t(mi_ref[...], jnp.concatenate(lines, 0)).astype(BF)
        for part in range(2):
            o_v[part, :, first * RB : (first + 2) * RB] = image[part * bins : (part + 1) * bins]
        cols = pl.ds(first * RB, 2 * RB)
        sends.append(
            pltpu.make_async_copy(o_v.at[:, :, cols], out_hbm.at[:, :, cols], out_sem.at[first // 2])
        )
        sends[-1].start()
    for send in sends:
        send.wait()


def order_of(ranks):
    far = [k for k in range(ranks) if k >= ranks // 2]
    near = [k for k in reversed(range(ranks)) if 0 < k < ranks // 2]
    order = []
    while far or near:
        order += far[:2] + near[:1]
        far, near = far[2:], near[1:]
    return order


def vmem(count):
    return [pl.BlockSpec(memory_space=pltpu.VMEM)] * count


def local(echoes, range_reference, kernels, shifts, phase_index, centroid, azimuth_reference):
    ranks = lax.axis_size("range")
    pulses, samples = echoes.shape[1:]
    first, second = R1, samples // R1
    cells = samples // ranks
    blocks = cells // RB
    bins = ranks * pulses
    taps = kernels.shape[1]
    halves = bins // LANES
    q_rows = halves * blocks
    assert second == RB and pulses == 2 * SUB and bins % LANES == 0 and blocks % 2 == 0

    n1, n2 = np.arange(first), np.arange(second)
    e1 = real_form(unit(n1, n1, first, -1.0)).reshape(2 * first, 2 * first)
    t1 = turn(n1, n2, samples, -1.0) / math.sqrt(first)
    w2 = real_form(unit(n2, n2, second, -1.0)).transpose(2, 3, 0, 1).reshape(2 * second, 2 * second)
    w3 = real_form(unit(n2, n2, second, 1.0)).transpose(2, 3, 0, 1).reshape(2 * second, 2 * second)
    t3 = turn(n1, n2, samples, 1.0) / math.sqrt(second)
    e4 = real_form(unit(n1, n1, first, 1.0)).reshape(2, ranks, blocks, 2 * first)
    e4 = e4.transpose(1, 0, 2, 3).reshape(2 * first, 2 * first)
    rows = 2 * blocks * pulses + SUB
    sent = pl.pallas_call(
        functools.partial(compress_kernel, ranks),
        out_shape=[jax.ShapeDtypeStruct((rows, LANES), BF)] * ranks,
        in_specs=[pl.BlockSpec(memory_space=pltpu.SMEM)] + [pl.BlockSpec(memory_space=pltpu.HBM)] * 4,
        out_specs=vmem(ranks),
        scratch_shapes=[
            pltpu.VMEM((2, pulses, samples), BF),
            pltpu.VMEM((4, 2 * first, 2 * first), BF),
            pltpu.VMEM((4, first, second), F32),
            pltpu.VMEM((2, samples), F32),
            pltpu.VMEM((2 * first * (pulses + 1), second), F32),
            pltpu.VMEM((pulses * (2 * first + 1), second), F32),
            pltpu.VMEM((2 * first + SUB, second), F32),
            pltpu.SemaphoreType.DMA((8,)),
        ],
        compiler_params=pltpu.CompilerParams(vmem_limit_bytes=55375000),
        name="compress",
    )(
        lax.axis_index("range").astype(jnp.int32).reshape(1),
        echoes,
        np.stack([as_bf(e1), as_bf(w2), as_bf(w3), as_bf(e4)]),
        np.concatenate([planes(t1), planes(t3)]),
        range_reference,
    )

    arrived = [sent[0]] * ranks
    for k in order_of(ranks):
        arrived[k] = lax.ppermute(sent[k], "range", [(i, i ^ k) for i in range(ranks)])

    def spread(table):
        return table.reshape(blocks, halves, LANES).transpose(1, 0, 2).reshape(q_rows, LANES)

    f = np.arange(bins)
    k1, k2 = f % ranks, f // ranks
    r, p = np.arange(ranks), np.arange(pulses)
    ahead = (
        unit(k1, r, ranks, -1.0)[:, :, None]
        * (turn(k1, p, bins, -1.0) * unit(k2, p, pulses, -1.0))[:, None, :]
        / math.sqrt(bins)
    )
    ahead = real_form(ahead.reshape(bins, bins)).reshape(2 * bins, 2, ranks, pulses)
    ahead = ahead.transpose(0, 2, 1, 3).reshape(2 * bins, 2 * bins)
    behind = (
        unit(r, k1, ranks, 1.0)[:, None, :]
        * (turn(p, k1, bins, 1.0) * unit(p, k2, pulses, 1.0))[None, :, :]
        / math.sqrt(bins)
    )
    behind = real_form(behind.reshape(bins, bins)).reshape(2 * bins, 2 * bins)
    column = jnp.arange(2 * bins, dtype=jnp.int32)
    wanted = column ^ (lax.axis_index("range").astype(jnp.int32) * (2 * pulses))
    choose = (column[:, None] == wanted[None, :]).astype(BF)
    ahead = jnp.dot(as_bf(ahead), choose, preferred_element_type=F32).astype(BF)
    edge = np.zeros((SLOT, LANES))
    edge[: 2 * SUB, : 2 * SUB] = np.eye(2 * SUB)
    edge[2 * SUB : 3 * SUB, LANES - SUB :] = np.eye(SUB)
    span = LEFT + RB + 3 * SUB
    smem = pl.BlockSpec(memory_space=pltpu.SMEM)
    weights, turned = pl.pallas_call(
        params_kernel,
        out_shape=[
            jax.ShapeDtypeStruct((taps, q_rows, LANES), F32),
            jax.ShapeDtypeStruct((2, q_rows, LANES), F32),
        ],
        in_specs=vmem(1) + [smem, smem] + vmem(1),
        out_specs=vmem(2),
        compiler_params=pltpu.CompilerParams(vmem_limit_bytes=4 << 20),
        name="params",
    )(spread(phase_index), kernels, lax.rem(centroid, jnp.int32(bins)), azimuth_reference)
    return pl.pallas_call(
        functools.partial(focus_kernel, ranks),
        out_shape=jax.ShapeDtypeStruct((2, bins, cells), BF),
        in_specs=vmem(6 + ranks),
        out_specs=pl.BlockSpec(memory_space=pl.ANY),
        scratch_shapes=[
            pltpu.VMEM((span * (2 * q_rows + 1), LANES), F32),
            pltpu.VMEM((2 * bins, cells + LANES), BF),
            pltpu.VMEM((2, bins, cells), BF),
            pltpu.SemaphoreType.DMA((blocks // 2,)),
        ],
        compiler_params=pltpu.CompilerParams(vmem_limit_bytes=48 << 20),
        name="focus",
    )(*arrived, ahead, as_bf(behind), as_bf(edge), spread(shifts), weights, turned)


def solution(mesh):
    in_specs = (
        P("groups", "range", None),
        P(),
        P(),
        P("range", None),
        P("range", None),
        P("range"),
        P(None, "range", None),
    )
    out_specs = P("groups", None, "range")

    return jax.shard_map(local, mesh=mesh, in_specs=in_specs, out_specs=out_specs, check_vma=False)
```

```python
import functools
import math

import jax
import jax.numpy as jnp
import numpy as np
from jax import lax
from jax.experimental import pallas as pl
from jax.experimental.pallas import tpu as pltpu
from jax.sharding import PartitionSpec as P

R1 = 128
RB = 128
LANES = 128
SUB = 8
SLOT = 32
LEFT = 8
BF = jnp.bfloat16
F32 = jnp.float32
CHUNK = 4
AT_ONCE = 16


def rounded(values):
    return np.asarray(np.asarray(values, np.float32), BF).astype(np.float64)


def unit(rows, columns, length, orient):
    angles = 2.0 * math.pi / length * (np.outer(rows, columns) % length)
    return rounded(np.cos(angles)) + 1j * orient * rounded(np.sin(angles))


def turn(rows, columns, length, orient):
    angles = 2.0 * math.pi / length * (np.outer(rows, columns) % length)
    return np.exp(1j * orient * angles)


def real_form(matrix):
    return np.stack(
        [np.stack([matrix.real, -matrix.imag], 1), np.stack([matrix.imag, matrix.real], 1)], 0
    )


def as_bf(values):
    return np.asarray(np.asarray(values, np.float32), BF)


def planes(values):
    return np.asarray(np.stack([values.real, values.imag], 0), np.float32)


def dot(left, right):
    return jnp.dot(left, right, preferred_element_type=F32)


def dot_t(left, right):
    return lax.dot_general(left, right, (((1,), (1,)), ((), ())), preferred_element_type=F32)


def turned_by(values, table, axis, back=False):
    re, im = values
    tr, ti = table
    if back:
        real = (re * tr + im * ti).astype(BF)
        return jnp.concatenate([real, (im * tr - re * ti).astype(BF)], axis)
    return jnp.concatenate([(re * tr - im * ti).astype(BF), (re * ti + im * tr).astype(BF)], axis)


def compress_kernel(dests, me_ref, x_hbm, m_hbm, t_hbm, r_hbm, *refs):
    outs = refs[:dests]
    x_v, m_v, t_v, r_v, s_in, s_out, r_sq, in_sem = refs[dests:]
    me = me_ref[0]
    pulses = x_hbm.shape[1]
    samples = x_hbm.shape[2]
    first = R1
    second = samples // first
    blocks = first // dests
    scale = 1.0 / math.sqrt(first)
    gap_in = pulses + 1
    gap_out = 2 * first + 1
    parts = 2

    copies = []
    span = samples // parts
    for part in range(2):
        for k in range(parts):
            piece = pl.ds(k * span, span)
            copies.append(
                pltpu.make_async_copy(
                    x_hbm.at[part, :, piece], x_v.at[part, :, piece], in_sem.at[len(copies)]
                )
            )
    copies.append(pltpu.make_async_copy(m_hbm, m_v, in_sem.at[len(copies)]))
    copies.append(pltpu.make_async_copy(t_hbm, t_v, in_sem.at[len(copies)]))
    copies.append(pltpu.make_async_copy(r_hbm, r_v, in_sem.at[len(copies)]))
    for copy in copies:
        copy.start()

    for part in range(2):
        for k in range(parts):
            copies[part * parts + k].wait()
            for n1 in range(k * first // parts, (k + 1) * first // parts):
                row = (part * first + n1) * gap_in
                s_in[row : row + pulses, :] = x_v[part, :, n1 * second : (n1 + 1) * second].astype(
                    F32
                )
    copies[-3].wait()
    copies[-2].wait()

    copies[-1].wait()
    for k2 in range(second):
        r_sq[pl.ds(k2, 2, stride=second + 1), :] = r_v[:, k2 * first : (k2 + 1) * first]
    slots = []
    for part in range(2):
        row = part * (second + 1)
        slots.append(jnp.transpose(r_sq[row : row + second, :]) * (1.0 / math.sqrt(second)))
    for part in range(2):
        r_sq[part * first : (part + 1) * first, :] = slots[part]


    for group in range(0, pulses, AT_ONCE):
        lines = []
        for p in range(group, group + AT_ONCE):
            lines.append(
                jnp.concatenate(
                    [
                        s_in[pl.ds(part * first * gap_in + p, first, stride=gap_in), :].astype(BF)
                        for part in range(2)
                    ],
                    0,
                )
            )
        half = dot(m_v[0], jnp.concatenate(lines, 1))
        table = (t_v[0], t_v[1])
        rows = []
        for k in range(AT_ONCE):
            cols = slice(k * second, (k + 1) * second)
            rows.append(turned_by((half[:first, cols], half[first:, cols]), table, 1))
        spec = dot(jnp.concatenate(rows, 0), m_v[1])
        table = (r_sq[:first, :], r_sq[first : 2 * first, :])
        rows = []
        for k in range(AT_ONCE):
            here = spec[k * first : (k + 1) * first]
            rows.append(turned_by((here[:, :second], here[:, second:]), table, 1))
        back = dot(jnp.concatenate(rows, 0), m_v[2])
        table = (t_v[0], t_v[1])
        lines = []
        for k in range(AT_ONCE):
            here = back[k * first : (k + 1) * first]
            lines.append(turned_by((here[:, :second], here[:, second:]), table, 0, True))
        done = dot(m_v[3], jnp.concatenate(lines, 1))
        for k in range(AT_ONCE):
            row = (group + k) * gap_out
            s_out[row : row + 2 * first, :] = done[:, k * second : (k + 1) * second] * scale

    def tile(dest, part, block):
        return s_out[pl.ds((dest * 2 + part) * blocks + block, pulses, stride=gap_out), :]

    lane = lax.broadcasted_iota(jnp.int32, (SUB, LANES), 1)
    for k in reversed(range(dests)):
        dest = me ^ k
        for part in range(2):
            for block in range(blocks):
                row = (part * blocks + block) * pulses
                outs[k][row : row + pulses, :] = tile(dest, part, block).astype(BF)
        halo = jnp.zeros((SUB, LANES), F32)
        take = (lane < 2 * SUB) & (dest + 1 < dests)
        give = (lane >= LANES - 3) & (dest > 0)
        for part in range(2):
            after = tile(jnp.minimum(dest + 1, dests - 1), part, 0)
            before = tile(jnp.maximum(dest - 1, 0), part, blocks - 1)
            for h in range(pulses // SUB):
                rows = slice(h * SUB, (h + 1) * SUB)
                piece = jnp.where(take, after[rows], jnp.where(give, before[rows], 0.0))
                slot = part * (pulses // SUB) + h
                halo = halo + (pltpu.roll(piece, SLOT * slot, 1) if slot else piece)
        row = 2 * blocks * pulses
        outs[k][row : row + SUB, :] = halo.astype(BF)


def params_kernel(ph_ref, k_ref, c_ref, a_ref, w_ref, t_ref):
    phases, taps = k_ref.shape
    blocks = a_ref.shape[1]
    phase = ph_ref[...]
    weights = [jnp.zeros(phase.shape, F32) for _ in range(taps)]
    for q in range(phases):
        hit = phase == q
        for t in range(taps):
            weights[t] = jnp.where(hit, k_ref[q, t], weights[t])
    for t in range(taps):
        w_ref[t] = weights[t]
    for part in range(2):
        for b in range(blocks):
            line = pltpu.roll(a_ref[part, b : b + 1, :], c_ref[b], 1)
            for h in range(phase.shape[0] // blocks):
                q = h * blocks + b
                t_ref[part, q : q + 1, :] = line[:, h * LANES : (h + 1) * LANES]


def focus_kernel(sources, *refs):
    y_refs = refs[:sources]
    mf_ref, mi_ref, edge_ref, s_ref, w_ref, a_ref = refs[sources : sources + 6]
    out_hbm, x_ref, d_ref, o_v, out_sem = refs[sources + 6 :]
    bins = out_hbm.shape[1]
    cells = out_hbm.shape[2]
    blocks = cells // RB
    pulses = bins // sources
    taps = w_ref.shape[0]
    halves = bins // LANES
    q_rows = halves * blocks
    stride = 2 * q_rows + 1
    lead = taps // 2 - 1

    def put(jj, count, part, h, b, values):
        x_ref[pl.ds(jj * stride + part * q_rows + h * blocks + b, count, stride=stride), :] = values

    own = []
    for b in range(blocks):
        own.append(
            jnp.concatenate(
                [
                    y[(o * blocks + b) * pulses : (o * blocks + b + 1) * pulses, :]
                    for y in y_refs
                    for o in range(2)
                ],
                0,
            )
        )
    side = []
    for y in y_refs:
        held = y[2 * blocks * pulses : 2 * blocks * pulses + SUB, :].astype(F32)
        for o in range(2):
            for h in range(pulses // SUB):
                slot = o * (pulses // SUB) + h
                side.append(pltpu.roll(held, LANES - SLOT * slot, 1) if slot else held)
    own.append(jnp.concatenate(side, 0).astype(BF))
    d_ref[...] = dot(mf_ref[...], jnp.concatenate(own, 1)).astype(BF)
    for b in range(blocks):
        for part in range(2):
            for h in range(halves):
                row = part * bins + h * LANES
                here = jnp.transpose(d_ref[row : row + LANES, b * RB : (b + 1) * RB]).astype(F32)
                put(LEFT, RB, part, h, b, here)
                if b > 0:
                    put(LEFT + RB, 2 * SUB, part, h, b - 1, here[: 2 * SUB])
                if b + 1 < blocks:
                    put(0, LEFT, part, h, b + 1, here[RB - LEFT :])
    turned = dot_t(edge_ref[...], d_ref[:, cells:])
    for part in range(2):
        for h in range(halves):
            col = part * bins + h * LANES
            put(LEFT + RB, 2 * SUB, part, h, blocks - 1, turned[: 2 * SUB, col : col + LANES])
            put(0, LEFT, part, h, 0, turned[2 * SUB : 3 * SUB, col : col + LANES])

    high = 2 * SUB
    for g in range(q_rows // high):
        shift = s_ref[g * high : (g + 1) * high, :].astype(jnp.int16)
        weights = [w_ref[t, g * high : (g + 1) * high, :].astype(BF) for t in range(taps)]
        ar, ai = [a_ref[part, g * high : (g + 1) * high, :].astype(BF) for part in range(2)]
        bits = [(shift & (1 << k)) != 0 for k in range(4)]
        seen = [[{} for _ in range(5)] for _ in range(2)]

        def moved(part, level, i):
            here = seen[part][level]
            if i not in here:
                if level == 0:
                    row = (i + LEFT - lead) * stride + part * q_rows + g * high
                    here[i] = x_ref[row : row + high, :].astype(BF)
                else:
                    step = 1 << (level - 1)
                    here[i] = jnp.where(
                        bits[level - 1], moved(part, level - 1, i + step), moved(part, level - 1, i)
                    )
            return here[i]

        for first in range(0, RB, CHUNK):
            sums = []
            for part in range(2):
                for j in range(first, first + CHUNK):
                    total = weights[0] * moved(part, 4, j)
                    for t in range(1, taps):
                        total = total + weights[t] * moved(part, 4, j + t)
                    sums.append(total)
            for k in range(CHUNK):
                re, im = sums[k], sums[CHUNK + k]
                row = (first + k) * stride + g * high
                x_ref[row : row + high, :] = (re * ar - im * ai).astype(F32)
                row += q_rows
                x_ref[row : row + high, :] = (re * ai + im * ar).astype(F32)

    sends = []
    for first in range(0, blocks, 2):
        lines = []
        for b in range(first, first + 2):
            lines.append(
                jnp.concatenate(
                    [
                        x_ref[pl.ds(part * q_rows + h * blocks + b, RB, stride=stride), :].astype(BF)
                        for part in range(2)
                        for h in range(halves)
                    ],
                    1,
                )
            )
        image = dot_t(mi_ref[...], jnp.concatenate(lines, 0)).astype(BF)
        for part in range(2):
            o_v[part, :, first * RB : (first + 2) * RB] = image[part * bins : (part + 1) * bins]
        cols = pl.ds(first * RB, 2 * RB)
        sends.append(
            pltpu.make_async_copy(o_v.at[:, :, cols], out_hbm.at[:, :, cols], out_sem.at[first // 2])
        )
        sends[-1].start()
    for send in sends:
        send.wait()


def order_of(ranks):
    far = [k for k in range(ranks) if k >= ranks // 2]
    near = [k for k in reversed(range(ranks)) if 0 < k < ranks // 2]
    order = []
    while far or near:
        order += far[:2] + near[:1]
        far, near = far[2:], near[1:]
    return order


def vmem(count):
    return [pl.BlockSpec(memory_space=pltpu.VMEM)] * count


def local(echoes, range_reference, kernels, shifts, phase_index, centroid, azimuth_reference):
    ranks = lax.axis_size("range")
    pulses, samples = echoes.shape[1:]
    first, second = R1, samples // R1
    cells = samples // ranks
    blocks = cells // RB
    bins = ranks * pulses
    taps = kernels.shape[1]
    halves = bins // LANES
    q_rows = halves * blocks
    assert second == RB and pulses == 2 * SUB and bins % LANES == 0 and blocks % 2 == 0

    n1, n2 = np.arange(first), np.arange(second)
    e1 = real_form(unit(n1, n1, first, -1.0)).reshape(2 * first, 2 * first)
    t1 = turn(n1, n2, samples, -1.0) / math.sqrt(first)
    w2 = real_form(unit(n2, n2, second, -1.0)).transpose(2, 3, 0, 1).reshape(2 * second, 2 * second)
    w3 = real_form(unit(n2, n2, second, 1.0)).transpose(2, 3, 0, 1).reshape(2 * second, 2 * second)
    e4 = real_form(unit(n1, n1, first, 1.0)).reshape(2, ranks, blocks, 2 * first)
    e4 = e4.transpose(1, 0, 2, 3).reshape(2 * first, 2 * first)
    rows = 2 * blocks * pulses + SUB
    sent = pl.pallas_call(
        functools.partial(compress_kernel, ranks),
        out_shape=[jax.ShapeDtypeStruct((rows, LANES), BF)] * ranks,
        in_specs=[pl.BlockSpec(memory_space=pltpu.SMEM)] + [pl.BlockSpec(memory_space=pltpu.HBM)] * 4,
        out_specs=vmem(ranks),
        scratch_shapes=[
            pltpu.VMEM((2, pulses, samples), BF),
            pltpu.VMEM((4, 2 * first, 2 * first), BF),
            pltpu.VMEM((2, first, second), F32),
            pltpu.VMEM((2, samples), F32),
            pltpu.VMEM((2 * first * (pulses + 1), second), F32),
            pltpu.VMEM((pulses * (2 * first + 1), second), F32),
            pltpu.VMEM((2 * first + SUB, second), F32),
            pltpu.SemaphoreType.DMA((8,)),
        ],
        compiler_params=pltpu.CompilerParams(vmem_limit_bytes=55375000),
        name="compress",
    )(
        lax.axis_index("range").astype(jnp.int32).reshape(1),
        echoes,
        np.stack([as_bf(e1), as_bf(w2), as_bf(w3), as_bf(e4)]),
        planes(t1),
        range_reference,
    )

    arrived = [sent[0]] * ranks
    for k in order_of(ranks):
        arrived[k] = lax.ppermute(sent[k], "range", [(i, i ^ k) for i in range(ranks)])

    def spread(table):
        return table.reshape(blocks, halves, LANES).transpose(1, 0, 2).reshape(q_rows, LANES)

    f = np.arange(bins)
    k1, k2 = f % ranks, f // ranks
    r, p = np.arange(ranks), np.arange(pulses)
    ahead = (
        unit(k1, r, ranks, -1.0)[:, :, None]
        * (turn(k1, p, bins, -1.0) * unit(k2, p, pulses, -1.0))[:, None, :]
        / math.sqrt(bins)
    )
    ahead = real_form(ahead.reshape(bins, bins)).reshape(2 * bins, 2, ranks, pulses)
    ahead = ahead.transpose(0, 2, 1, 3).reshape(2 * bins, 2 * bins)
    behind = (
        unit(r, k1, ranks, 1.0)[:, None, :]
        * (turn(p, k1, bins, 1.0) * unit(p, k2, pulses, 1.0))[None, :, :]
        / math.sqrt(bins)
    )
    behind = real_form(behind.reshape(bins, bins)).reshape(2 * bins, 2 * bins)
    column = jnp.arange(2 * bins, dtype=jnp.int32)
    wanted = column ^ (lax.axis_index("range").astype(jnp.int32) * (2 * pulses))
    choose = (column[:, None] == wanted[None, :]).astype(BF)
    ahead = jnp.dot(as_bf(ahead), choose, preferred_element_type=F32).astype(BF)
    edge = np.zeros((SLOT, LANES))
    edge[: 2 * SUB, : 2 * SUB] = np.eye(2 * SUB)
    edge[2 * SUB : 3 * SUB, LANES - SUB :] = np.eye(SUB)
    span = LEFT + RB + 3 * SUB
    smem = pl.BlockSpec(memory_space=pltpu.SMEM)
    weights, turned = pl.pallas_call(
        params_kernel,
        out_shape=[
            jax.ShapeDtypeStruct((taps, q_rows, LANES), F32),
            jax.ShapeDtypeStruct((2, q_rows, LANES), F32),
        ],
        in_specs=vmem(1) + [smem, smem] + vmem(1),
        out_specs=vmem(2),
        compiler_params=pltpu.CompilerParams(vmem_limit_bytes=4 << 20),
        name="params",
    )(spread(phase_index), kernels, lax.rem(centroid, jnp.int32(bins)), azimuth_reference)
    return pl.pallas_call(
        functools.partial(focus_kernel, ranks),
        out_shape=jax.ShapeDtypeStruct((2, bins, cells), BF),
        in_specs=vmem(6 + ranks),
        out_specs=pl.BlockSpec(memory_space=pl.ANY),
        scratch_shapes=[
            pltpu.VMEM((span * (2 * q_rows + 1), LANES), F32),
            pltpu.VMEM((2 * bins, cells + LANES), BF),
            pltpu.VMEM((2, bins, cells), BF),
            pltpu.SemaphoreType.DMA((blocks // 2,)),
        ],
        compiler_params=pltpu.CompilerParams(vmem_limit_bytes=48 << 20),
        name="focus",
    )(*arrived, ahead, as_bf(behind), as_bf(edge), spread(shifts), weights, turned)


def solution(mesh):
    in_specs = (
        P("groups", "range", None),
        P(),
        P(),
        P("range", None),
        P("range", None),
        P("range"),
        P(None, "range", None),
    )
    out_specs = P("groups", None, "range")

    return jax.shard_map(local, mesh=mesh, in_specs=in_specs, out_specs=out_specs, check_vma=False)
```
